32 devices in a mesh: groups: 1, wa: 32 (over z, y, x, core).
Axes of the slice: x: 2, y: 2, z: 4, core: 2. Of those that a mesh axis runs over, the one named last changes fastest.
Arguments:
- queries: bfloat16 [32, 1, 384, 1536], P(('groups', 'wa')), may hold values from -10 to 10
- keys_values: bfloat16 [2, 32, 1, 384, 1536], P(None, ('groups', 'wa')), may hold values from -10 to 10
- tile_visible: int32 [32, 1], P('groups'), may hold values 0 or 1
- out_weight: bfloat16 [1536, 3072], P(None, 'wa'), may hold values from -0.15625 to 0.15625
Outputs:
- mixed: bfloat16 [32, 1, 384, 3072], P(('groups', 'wa'))
The draws below stay inside these ranges and needn't reach their ends.
All inputs are finite; a program needn't handle non-finite values.
Results may differ from the reference program's by a relative error of at most 0.0057.
Values may be sent and summed in bfloat16 or wider, within the bound.
No kernel may reach another device: no remote copies, remote signals or barrier semaphores. Data moves between devices by JAX's collectives and lax.ppermute only.
A program may use at most 128 MiB of HBM per device.

```python
import jax
import jax.numpy as jnp
from jax import lax

HEADS = 12
HEAD_DIM = 128
D = 3072
TILE = 384
GW = 8
TIME_TILES = 1
HALL = 1536
N_WA = 32


def base_field(key, grid_shape):
    return jax.random.truncated_normal(key, -4.0, 4.0, grid_shape, jnp.float32)


def draw_queries(key, part):
    grid_shape = (N_WA, TIME_TILES, TILE, HALL)
    drawn = base_field(jax.random.fold_in(key, 11), grid_shape)
    return drawn.astype(jnp.bfloat16)


def draw_keys_values(key, part):
    grid_shape = (N_WA, TIME_TILES, TILE, HALL)
    key_part = base_field(jax.random.fold_in(key, 12), grid_shape)
    value_part = base_field(jax.random.fold_in(key, 13), grid_shape)
    return jnp.stack([key_part, value_part]).astype(jnp.bfloat16)


def set_ends(array, own_key, smallest, largest):
    shape = array.shape
    spot = [jax.random.randint(jax.random.fold_in(own_key, axis), (), 0, shape[axis]) for axis in range(len(shape))]
    array = array.at[tuple(spot)].set(smallest)
    longest = shape.index(max(shape))
    spot[longest] = (spot[longest] + 1) % shape[longest]
    return array.at[tuple(spot)].set(largest)


def shard_levels(stream_key, extent, shards, least, high):
    def one(position, blocks):
        steps = jax.random.uniform(jax.random.fold_in(jax.random.fold_in(stream_key, 6), position), (blocks,), jnp.float32, least / len(shards), high / len(shards))
        return jnp.repeat(jnp.exp(steps), extent[position] // blocks).reshape((-1,) + (1,) * (len(extent) - position - 1))

    gain = one(*shards[0])
    for cut in shards[1:]:
        gain = gain * one(*cut)
    return gain


def normal_values(stream_key, extent, scale, reach, shards=(), held_as=jnp.bfloat16):
    values = jax.random.normal(stream_key, extent, jnp.float32) * scale
    if len(shards) > 0:
        values = shard_levels(stream_key, extent, shards, -0.22, 0.18) * values
    return jnp.clip(values, min=-reach, max=reach).astype(held_as)


def setup_inputs(seed: int = 0, part: int = 0) -> dict:
    seeds = jax.random.split(jax.random.key(seed), 5)
    part_keys = jax.random.split(jax.random.fold_in(seeds[4], part), 5)
    return {
        "queries": draw_queries(jax.random.fold_in(jax.random.fold_in(seeds[4], part), 71), part),
        "keys_values": draw_keys_values(jax.random.fold_in(jax.random.fold_in(seeds[4], part), 71), part),
        "tile_visible": set_ends((jax.random.randint(part_keys[2], (N_WA, TIME_TILES), 0, 4) < 3).astype(jnp.int32), jax.random.fold_in(part_keys[2], 1), 0, 1),
        "out_weight": normal_values(seeds[3], (HALL, D), HALL ** -0.5, 0.15625, ((1, 32),)),
    }


window_offsets = ((-1, -1), (-1, 0), (-1, 1), (0, -1), (0, 0), (0, 1), (1, -1), (1, 0), (1, 1))


def column_window(keys_values, tile_visible, column):
    grid_rows = N_WA // GW
    tile_row = column // GW
    tile_col = column % GW
    pieces = []
    visible_flags = []
    for step_row, step_col in window_offsets:
        near_row = tile_row + step_row
        near_col = tile_col + step_col
        inside = (near_row >= 0) & (near_row < grid_rows) & (near_col >= 0) & (near_col < GW)
        source = (jnp.clip(near_row, 0, grid_rows - 1) * GW + jnp.clip(near_col, 0, GW - 1)).astype(jnp.int32)
        pieces.append(lax.dynamic_index_in_dim(keys_values, source, 1, keepdims=False))
        marked = lax.dynamic_index_in_dim(tile_visible, source, 0, keepdims=False) == 1
        if step_row == 0 and step_col == 0:
            visible_flags.append(jnp.broadcast_to(inside, marked.shape))
        else:
            visible_flags.append(inside & marked)
    window = jnp.stack(pieces, axis=2)
    window = window.reshape(2, TIME_TILES, 9 * TILE, HALL)
    flags = jnp.stack(visible_flags, axis=1)
    key_keep = jnp.broadcast_to(flags[:, :, None], (TIME_TILES, 9, TILE)).reshape(TIME_TILES, 9 * TILE)
    return window, key_keep


def reference(queries, keys_values, tile_visible, out_weight):
    score_scale = HEAD_DIM ** -0.5

    def one_column(column):
        window, key_keep = column_window(keys_values, tile_visible, column)
        query_block = lax.dynamic_index_in_dim(queries, column, 0, keepdims=False)
        query_heads = query_block.astype(jnp.float32).reshape(TIME_TILES, TILE, HEADS, HEAD_DIM)
        key_heads = window[0].astype(jnp.float32).reshape(TIME_TILES, 9 * TILE, HEADS, HEAD_DIM)
        value_heads = window[1].astype(jnp.float32).reshape(TIME_TILES, 9 * TILE, HEADS, HEAD_DIM)
        scores = jnp.einsum("tqhd,tkhd->thqk", query_heads, key_heads) * score_scale
        keep_wide = key_keep[:, None, None, :]
        scores = jnp.where(keep_wide, scores, -1e30)
        row_max = jnp.max(scores, axis=3, keepdims=True)
        weights = jnp.where(keep_wide, jnp.exp(scores - row_max), 0.0)
        row_total = jnp.sum(weights, axis=3)
        weights_low = weights.astype(jnp.bfloat16).astype(jnp.float32)
        summed = jnp.einsum("thqk,tkhd->tqhd", weights_low, value_heads)
        attended = summed / jnp.transpose(row_total, (0, 2, 1))[..., None]
        attended = attended.astype(jnp.bfloat16).reshape(TIME_TILES * TILE, HALL)
        projected = jnp.dot(attended, out_weight, preferred_element_type=jnp.float32)
        return projected.astype(jnp.bfloat16).reshape(TIME_TILES, TILE, D)

    return lax.map(one_column, jnp.arange(N_WA, dtype=jnp.int32))
```

```python
import functools
import math

import jax
import jax.numpy as jnp
from jax import lax
from jax.experimental import pallas as pl
from jax.experimental.pallas import tpu as pltpu
from jax.sharding import PartitionSpec as P

HEAD_DIM = 128
GW = 8
CHUNKS = (3, 3, 3, 3)
STAT_ROWS = 16
BIG = 1e30


def pair_swaps(count, stride, parity, block):
    pairs = []
    for device in range(count):
        position = (device // stride) % block
        if position % 2 == parity % 2 and position + 1 < block:
            pairs.append((device, device + stride))
            pairs.append((device + stride, device))
    return pairs


def column_to_row(column):
    size = column.shape[0]
    same = lax.broadcasted_iota(jnp.int32, (size, size), 0) == lax.broadcasted_iota(jnp.int32, (size, size), 1)
    return jnp.sum(jnp.where(same, column, 0.0), axis=0, keepdims=True)


def row_to_column(row):
    size = row.shape[1]
    same = lax.broadcasted_iota(jnp.int32, (size, size), 0) == lax.broadcasted_iota(jnp.int32, (size, size), 1)
    return jnp.sum(jnp.where(same, row, 0.0), axis=1, keepdims=True)


def split_three(value):
    high = value.astype(jnp.bfloat16)
    rest = value - high.astype(jnp.float32)
    middle = rest.astype(jnp.bfloat16)
    low = (rest - middle.astype(jnp.float32)).astype(jnp.bfloat16)
    return high, middle, low


def attend_kernel(flags, q_own, q_even, q_odd, kv_own, kv_even, kv_odd, out_own, out_even, out_odd):
    tile = q_own.shape[0]
    block = 128
    factor = HEAD_DIM ** (-0.5) * math.log2(math.e)
    keys = jnp.concatenate([kv_own[0], kv_even[0], kv_odd[0]], axis=0)
    values = jnp.concatenate([kv_own[1], kv_even[1], kv_odd[1]], axis=0)
    for place, (q_ref, out_ref) in enumerate(((q_own, out_own), (q_even, out_even), (q_odd, out_odd))):
        seen = (flags[0] if place == 0 else flags[1], flags[2], flags[3])
        stats = []
        for start in range(0, tile, block):
            query = q_ref[start : start + block, :]
            scores = lax.dot_general(query, keys, (((1,), (1,)), ((), ())), preferred_element_type=jnp.float32)
            parts = [scores[:, i * tile : (i + 1) * tile] for i in range(3)]
            peaks = [
                jnp.where(seen[i] == 1, jnp.max(parts[i], axis=1, keepdims=True) * factor, -BIG) for i in range(3)
            ]
            peak = jnp.maximum(jnp.maximum(peaks[0], peaks[1]), peaks[2])
            weights = [jnp.exp2(parts[i] * factor - jnp.where(seen[i] == 1, peak, BIG)) for i in range(3)]
            total = sum(jnp.sum(w, axis=1, keepdims=True) for w in weights)
            low = jnp.concatenate([w.astype(jnp.bfloat16) for w in weights], axis=1)
            summed = jnp.dot(low, values, preferred_element_type=jnp.float32)
            some = total > 0.0
            safe = jnp.where(some, total, 1.0)
            out_ref[start : start + block, :] = (summed / safe).astype(out_ref.dtype)
            stats.append(column_to_row(jnp.where(some, peak + jnp.log2(safe), -BIG)))
        stat = jnp.concatenate(stats, axis=0)
        rows = stat.shape[0]
        if out_ref.dtype == jnp.float32:
            out_ref[tile : tile + rows, :] = stat
            out_ref[tile + rows : tile + STAT_ROWS, :] = jnp.zeros((STAT_ROWS - rows, block), jnp.float32)
        else:
            pieces = list(split_three(stat)) + [jnp.zeros((STAT_ROWS - 3 * rows, block), jnp.bfloat16)]
            packed = jnp.concatenate([p.astype(jnp.float32) for p in pieces], axis=0)
            out_ref[tile : tile + STAT_ROWS, :] = packed.astype(jnp.bfloat16)


def attend(flags, queries, kv_own, kv_near, first_head, heads):
    tile = kv_own.shape[1]
    q_spec = pl.BlockSpec((tile, HEAD_DIM), lambda h, f: (0, first_head + h))
    own_spec = pl.BlockSpec((2, tile, HEAD_DIM), lambda h, f: (0, 0, first_head + h))
    near_spec = pl.BlockSpec((2, tile, HEAD_DIM), lambda h, f: (0, 0, h))
    out_spec = pl.BlockSpec((tile + STAT_ROWS, HEAD_DIM), lambda h, f: (0, h))
    shape = (tile + STAT_ROWS, heads * HEAD_DIM)
    pair_count = 9 * tile * tile * heads
    return pl.pallas_call(
        attend_kernel,
        grid_spec=pltpu.PrefetchScalarGridSpec(
            num_scalar_prefetch=1,
            grid=(heads,),
            in_specs=[q_spec] * 3 + [own_spec] + [near_spec] * 2,
            out_specs=[out_spec] * 3,
        ),
        out_shape=[
            jax.ShapeDtypeStruct(shape, jnp.float32),
            jax.ShapeDtypeStruct(shape, jnp.bfloat16),
            jax.ShapeDtypeStruct(shape, jnp.bfloat16),
        ],
        cost_estimate=pl.CostEstimate(
            flops=pair_count * HEAD_DIM * 4,
            transcendentals=pair_count,
            bytes_accessed=heads * HEAD_DIM * tile * 2 * 13,
        ),
        name="attend",
    )(flags, *queries, kv_own, *kv_near)


def merge_kernel(edge, own, even, odd, attended):
    tile = attended.shape[0]
    block = 128
    rows = tile // block
    own_stat = own[tile : tile + STAT_ROWS, :]
    near_stats = [ref[tile : tile + STAT_ROWS, :].astype(jnp.float32) for ref in (even, odd)]
    for i in range(rows):
        levels = [row_to_column(own_stat[i : i + 1, :])]
        for stat in near_stats:
            joined = stat[i : i + 1, :] + stat[rows + i : rows + i + 1, :] + stat[2 * rows + i : 2 * rows + i + 1, :]
            levels.append(row_to_column(joined))
        levels[2] = jnp.where(edge[0] == 1, -BIG, levels[2])
        top = jnp.maximum(jnp.maximum(levels[0], levels[1]), levels[2])
        shares = [jnp.exp2(level - top) for level in levels]
        scale = 1.0 / (shares[0] + shares[1] + shares[2])
        span = slice(i * block, (i + 1) * block)
        mixed = (
            own[span, :] * (shares[0] * scale)
            + even[span, :].astype(jnp.float32) * (shares[1] * scale)
            + odd[span, :].astype(jnp.float32) * (shares[2] * scale)
        )
        attended[span, :] = mixed.astype(jnp.bfloat16)


def merge(edge, own, even, odd):
    tile = own.shape[0] - STAT_ROWS
    heads = own.shape[1] // HEAD_DIM
    spec = pl.BlockSpec((tile + STAT_ROWS, HEAD_DIM), lambda h, e: (0, h))
    return pl.pallas_call(
        merge_kernel,
        grid_spec=pltpu.PrefetchScalarGridSpec(
            num_scalar_prefetch=1,
            grid=(heads,),
            in_specs=[spec] * 3,
            out_specs=pl.BlockSpec((tile, HEAD_DIM), lambda h, e: (0, h)),
        ),
        out_shape=jax.ShapeDtypeStruct((tile, heads * HEAD_DIM), jnp.bfloat16),
        cost_estimate=pl.CostEstimate(
            flops=tile * heads * HEAD_DIM * 8, transcendentals=0, bytes_accessed=tile * heads * HEAD_DIM * 10
        ),
        name="merge",
    )(edge, own, even, odd)


def project_kernel(piece_masks, shard, group, *refs):
    count = len(piece_masks)
    pieces = refs[:count]
    att_refs = refs[count:-3]
    out_ref, held, sem = refs[-3:]
    step = pl.program_id(0)
    me = lax.axis_index("wa")
    sources = [(ref, place, mask) for ref, masks in zip(pieces, piece_masks) for place, mask in enumerate(masks)]

    def copy(ref, place, mask):
        owner = jnp.bitwise_xor(me, mask)
        target = pl.ds(pl.multiple_of(owner * shard, shard), shard)
        return pltpu.make_async_copy(
            ref.at[pl.ds(place * shard, shard)], held.at[target], sem.at[owner]
        )

    @pl.when(step == 0)
    def _():
        for source in sources:
            copy(*source).start()

    for i in range(group):
        owner = step * group + i
        target = pl.ds(pl.multiple_of(owner * shard, shard), shard)
        pltpu.make_async_copy(pieces[0].at[pl.ds(0, shard)], held.at[target], sem.at[owner]).wait()
    columns = pl.ds(pl.multiple_of(step * (group * shard), 128), group * shard)
    depth = 0
    total = None
    for ref in att_refs:
        width = ref.shape[1]
        part = lax.dot_general(
            ref[...],
            held[columns, depth : depth + width],
            (((1,), (1,)), ((), ())),
            preferred_element_type=jnp.float32,
        )
        total = part if total is None else total + part
        depth += width
    out_ref[...] = total.astype(jnp.bfloat16)


def project(attended, pieces, piece_masks, shard, count):
    tile = attended[0].shape[0]
    depth = pieces[0].shape[1]
    group = 128 // math.gcd(128, shard)
    return pl.pallas_call(
        functools.partial(project_kernel, piece_masks, shard, group),
        grid=(count // group,),
        in_specs=[pl.BlockSpec(memory_space=pl.ANY)] * len(pieces)
        + [pl.BlockSpec(a.shape, lambda g: (0, 0)) for a in attended],
        out_specs=pl.BlockSpec((tile, group * shard), lambda g: (0, g)),
        out_shape=jax.ShapeDtypeStruct((tile, count * shard), jnp.bfloat16),
        scratch_shapes=[pltpu.VMEM((count * shard, depth), jnp.bfloat16), pltpu.SemaphoreType.DMA((count,))],
        cost_estimate=pl.CostEstimate(
            flops=2 * tile * depth * count * shard, transcendentals=0, bytes_accessed=2 * depth * count * shard
        ),
        name="project",
    )(*pieces, *attended)


def gather_weight(own, count):
    bits = [b for b in (8 << k for k in range(20)) if b < count] + [b for b in (2, 4, 1) if b < count]
    pieces, masks = [own], [(0,)]
    for bit in bits:
        swap = [(device, device ^ bit) for device in range(count)]
        joined = pieces[0] if len(pieces) == 1 else jnp.concatenate(pieces, axis=0)
        held = tuple(m for group in masks for m in group)
        pieces.append(lax.ppermute(joined, "wa", swap))
        masks.append(tuple(m ^ bit for m in held))
    return pieces, masks


def local(queries, keys_values, tile_visible, out_weight):
    count = lax.axis_size("wa")
    grid_rows = count // GW
    me = lax.axis_index("wa")
    row, col = me // GW, me % GW
    time_tiles, tile, width = queries.shape[1:]
    shard = out_weight.shape[1]

    row_even, row_odd = (pair_swaps(count, GW, parity, grid_rows) for parity in (0, 1))
    col_even, col_odd = (pair_swaps(count, 1, parity, GW) for parity in (0, 1))

    def partner(position, parity, limit):
        near = jnp.where(position % 2 == parity, position + 1, position - 1)
        return jnp.clip(near, 0, limit - 1), (near >= 0) & (near < limit)

    near_even, inside_even = partner(row, 0, grid_rows)
    near_odd, inside_odd = partner(row, 1, grid_rows)

    doubling = count & (count - 1) == 0 and shard % 16 == 0 and count % (128 // math.gcd(128, shard)) == 0
    if doubling:
        pieces, masks = gather_weight(out_weight.T, count)
    else:
        whole = lax.all_gather(out_weight, "wa", axis=1, tiled=True)

    outputs = []
    for t in range(time_tiles):
        marked = tile_visible[:, t]
        flags = jnp.stack(
            [
                jnp.int32(1),
                (marked[me] == 1).astype(jnp.int32),
                (inside_even & (marked[near_even * GW + col] == 1)).astype(jnp.int32),
                (inside_odd & (marked[near_odd * GW + col] == 1)).astype(jnp.int32),
            ]
        )
        query = queries[0, t]
        kv_own = keys_values[:, 0, t]
        near_queries = [lax.ppermute(query, "wa", swap) for swap in (col_even, col_odd)]
        first = 0
        partial = []
        for heads in CHUNKS:
            cut = kv_own[:, :, first * HEAD_DIM : (first + heads) * HEAD_DIM]
            kv_near = [lax.ppermute(cut, "wa", swap) for swap in (row_even, row_odd)]
            partial.append((first, heads, kv_near))
            first += heads
        attended = []
        edge = (col == 0) | (col == GW - 1)
        for first, heads, kv_near in partial:
            own, even, odd = attend(flags, [query] + near_queries, kv_own, kv_near, first, heads)
            even = lax.ppermute(even, "wa", col_even)
            odd = lax.ppermute(odd, "wa", col_odd)
            attended.append(merge(edge.astype(jnp.int32).reshape(1), own, even, odd))
        if doubling:
            outputs.append(project(attended, pieces, masks, shard, count))
        else:
            outputs.append(
                jnp.dot(
                    jnp.concatenate(attended, axis=1), whole, preferred_element_type=jnp.float32
                ).astype(jnp.bfloat16)
            )
    return jnp.stack(outputs)[None]


def solution(mesh):
    in_specs = (
        P(("groups", "wa"), None, None, None),
        P(None, ("groups", "wa"), None, None, None),
        P("groups", None),
        P(None, "wa"),
    )
    out_specs = P(("groups", "wa"), None, None, None)
    return jax.shard_map(local, mesh=mesh, in_specs=in_specs, out_specs=out_specs, check_vma=False)
```

```python
import functools
import math

import jax
import jax.numpy as jnp
from jax import lax
from jax.experimental import pallas as pl
from jax.experimental.pallas import tpu as pltpu
from jax.sharding import PartitionSpec as P


HEAD_DIM = 128
GW = 8
CHUNKS = 4
STAT_ROWS = 16
BIG = 1e30


def pair_swaps(count, stride, parity, block):
    pairs = []
    for device in range(count):
        position = (device // stride) % block
        if position % 2 == parity % 2 and position + 1 < block:
            pairs.append((device, device + stride))
            pairs.append((device + stride, device))
    return pairs


def split_three(value):
    high = value.astype(jnp.bfloat16)
    rest = value - high.astype(jnp.float32)
    middle = rest.astype(jnp.bfloat16)
    low = (rest - middle.astype(jnp.float32)).astype(jnp.bfloat16)
    return high, middle, low


def attend_kernel(flags, q_own, q_even, q_odd, kv_own, kv_even, kv_odd, out_own, out_even, out_odd):
    tile = q_own.shape[0]
    block = 128
    rows = tile // block
    factor = HEAD_DIM ** (-0.5) * math.log2(math.e)
    keys = jnp.concatenate([kv_own[0], kv_even[0], kv_odd[0]], axis=0)
    values = jnp.concatenate([kv_own[1], kv_even[1], kv_odd[1]], axis=0)
    values = jnp.concatenate([values, jnp.ones_like(values)], axis=1)
    places = ((q_own, out_own), (q_even, out_even), (q_odd, out_odd))
    diagonal = lax.broadcasted_iota(jnp.int32, (block, block), 0) == lax.broadcasted_iota(
        jnp.int32, (block, block), 1
    )

    def score(place, i):
        query = places[place][0][i * block : (i + 1) * block, :]
        return lax.dot_general(query, keys, (((1,), (1,)), ((), ())), preferred_element_type=jnp.float32)

    def finish(place, i, scores):
        out_ref = places[place][1]
        seen = (flags[0] if place == 0 else flags[1], flags[2], flags[3])
        parts = [scores[:, t * tile : (t + 1) * tile] for t in range(3)]
        peaks = [
            jnp.where(seen[t] == 1, jnp.max(parts[t], axis=1, keepdims=True) * factor, -BIG) for t in range(3)
        ]
        peak = jnp.maximum(jnp.maximum(peaks[0], peaks[1]), peaks[2])
        weights = [jnp.exp2(parts[t] * factor - jnp.where(seen[t] == 1, peak, BIG)) for t in range(3)]
        low = jnp.concatenate([w.astype(jnp.bfloat16) for w in weights], axis=1)
        summed = jnp.dot(low, values, preferred_element_type=jnp.float32)
        total = summed[:, HEAD_DIM:]
        some = total > 0.0
        safe = jnp.where(some, total, 1.0)
        out_ref[i * block : (i + 1) * block, :] = (summed[:, :HEAD_DIM] / safe).astype(out_ref.dtype)
        level = jnp.where(some, peak + jnp.log2(safe), -BIG)
        return jnp.sum(jnp.where(diagonal, level, 0.0), axis=0, keepdims=True)

    def store(place, stats):
        out_ref = places[place][1]
        stat = jnp.concatenate(stats, axis=0)
        if out_ref.dtype == jnp.float32:
            packed = [stat, jnp.zeros((STAT_ROWS - rows, block), jnp.float32)]
        else:
            packed = [p.astype(jnp.float32) for p in split_three(stat)]
            packed.append(jnp.zeros((STAT_ROWS - 3 * rows, block), jnp.float32))
        out_ref[tile : tile + STAT_ROWS, :] = jnp.concatenate(packed, axis=0).astype(out_ref.dtype)

    order = [(place, i) for place in range(3) for i in range(rows)]
    stats = {}
    ahead = score(*order[0])
    for n, (place, i) in enumerate(order):
        scores = ahead
        if n + 1 < len(order):
            ahead = score(*order[n + 1])
        stats.setdefault(place, []).append(finish(place, i, scores))
        if i == rows - 1:
            store(place, stats[place])


def attend(flags, queries, kv_own, kv_near, first_head, heads):
    tile = kv_own.shape[1]
    q_spec = pl.BlockSpec((tile, HEAD_DIM), lambda h, f: (0, first_head + h))
    own_spec = pl.BlockSpec((2, tile, HEAD_DIM), lambda h, f: (0, 0, first_head + h))
    near_spec = pl.BlockSpec((2, tile, HEAD_DIM), lambda h, f: (0, 0, h))
    out_spec = pl.BlockSpec((tile + STAT_ROWS, HEAD_DIM), lambda h, f: (0, h))
    shape = (tile + STAT_ROWS, heads * HEAD_DIM)
    pair_count = 9 * tile * tile * heads
    return pl.pallas_call(
        attend_kernel,
        grid_spec=pltpu.PrefetchScalarGridSpec(
            num_scalar_prefetch=1,
            grid=(heads,),
            in_specs=[q_spec] * 3 + [own_spec] + [near_spec] * 2,
            out_specs=[out_spec] * 3,
        ),
        out_shape=[
            jax.ShapeDtypeStruct(shape, jnp.float32),
            jax.ShapeDtypeStruct(shape, jnp.bfloat16),
            jax.ShapeDtypeStruct(shape, jnp.bfloat16),
        ],
        cost_estimate=pl.CostEstimate(
            flops=pair_count * HEAD_DIM * 4,
            transcendentals=pair_count,
            bytes_accessed=heads * HEAD_DIM * tile * 2 * 13,
        ),
        name="attend",
    )(flags, *queries, kv_own, *kv_near)


def merge_kernel(edge, own, even, odd, attended):
    tile = attended.shape[0]
    block = 128
    rows = tile // block
    levels = [own[tile : tile + rows, :]]
    for ref in (even, odd):
        stat = ref[tile : tile + STAT_ROWS, :].astype(jnp.float32)
        levels.append(stat[:rows] + stat[rows : 2 * rows] + stat[2 * rows : 3 * rows])
    levels[2] = jnp.where(edge[0] == 1, -BIG, levels[2])
    top = jnp.maximum(jnp.maximum(levels[0], levels[1]), levels[2])
    shares = [jnp.exp2(level - top) for level in levels]
    scale = 1.0 / (shares[0] + shares[1] + shares[2])
    for i in range(rows):
        span = slice(i * block, (i + 1) * block)
        mixed = None
        for ref, share in zip((own, even, odd), shares):
            wide = jnp.broadcast_to((share * scale)[i : i + 1, :], (block, block)).T
            part = ref[span, :].astype(jnp.float32) * wide
            mixed = part if mixed is None else mixed + part
        attended[span, :] = mixed.astype(jnp.bfloat16)


def merge(edge, own, even, odd):
    tile = own.shape[0] - STAT_ROWS
    heads = own.shape[1] // HEAD_DIM
    spec = pl.BlockSpec((tile + STAT_ROWS, HEAD_DIM), lambda h, e: (0, h))
    return pl.pallas_call(
        merge_kernel,
        grid_spec=pltpu.PrefetchScalarGridSpec(
            num_scalar_prefetch=1,
            grid=(heads,),
            in_specs=[spec] * 3,
            out_specs=pl.BlockSpec((tile, HEAD_DIM), lambda h, e: (0, h)),
        ),
        out_shape=jax.ShapeDtypeStruct((tile, heads * HEAD_DIM), jnp.bfloat16),
        cost_estimate=pl.CostEstimate(
            flops=tile * heads * HEAD_DIM * 8, transcendentals=0, bytes_accessed=tile * heads * HEAD_DIM * 10
        ),
        name="merge",
    )(edge, own, even, odd)


def project_kernel(masks, shard, group, edge_bit, *refs):
    count = len(masks)
    pieces = refs[:count]
    att_refs = refs[count:-3]
    out_ref, held, sem = refs[-3:]
    step = pl.program_id(0)
    me = lax.axis_index("wa")
    row = me // GW
    flip = jnp.where((row == 0) | (row == 3), edge_bit, 0)

    def move(ref, place, owner):
        target = pl.ds(pl.multiple_of(owner * shard, shard), shard)
        return pltpu.make_async_copy(ref.at[pl.ds(place * shard, shard)], held.at[target], sem.at[owner])

    @pl.when(step == 0)
    def _():
        for ref, mask in zip(pieces, masks):
            first = jnp.bitwise_xor(me, mask)
            if mask & (2 * GW):
                first = jnp.bitwise_xor(first, flip)
            for place in range(2):
                move(ref, place, jnp.bitwise_xor(first, place * GW)).start()

    for i in range(group):
        move(pieces[0], 0, step * group + i).wait()
    columns = pl.ds(pl.multiple_of(step * (group * shard), 128), group * shard)
    depth = 0
    total = None
    for ref in att_refs:
        width = ref.shape[1]
        part = lax.dot_general(
            ref[...],
            held[columns, depth : depth + width],
            (((1,), (1,)), ((), ())),
            preferred_element_type=jnp.float32,
        )
        total = part if total is None else total + part
        depth += width
    out_ref[...] = total.astype(jnp.bfloat16)


def project(attended, pieces, masks, shard, count):
    tile = attended[0].shape[0]
    depth = pieces[0].shape[1]
    group = 128 // math.gcd(128, shard)
    return pl.pallas_call(
        functools.partial(project_kernel, masks, shard, group, GW),
        grid=(count // group,),
        in_specs=[pl.BlockSpec(memory_space=pl.ANY)] * len(pieces)
        + [pl.BlockSpec(a.shape, lambda g: (0, 0)) for a in attended],
        out_specs=pl.BlockSpec((tile, group * shard), lambda g: (0, g)),
        out_shape=jax.ShapeDtypeStruct((tile, count * shard), jnp.bfloat16),
        scratch_shapes=[pltpu.VMEM((count * shard, depth), jnp.bfloat16), pltpu.SemaphoreType.DMA((count,))],
        cost_estimate=pl.CostEstimate(
            flops=2 * tile * depth * count * shard, transcendentals=0, bytes_accessed=2 * depth * count * shard
        ),
        name="project",
    )(*pieces, *attended)


def passed(value, pairs):
    return lax.ppermute(value, "wa", pairs)


def gather_weight(own, count, row_even, row_odd, edge_row):
    def swap(value, bit):
        return passed(value, [(device, device ^ bit) for device in range(count)])

    ab = jnp.concatenate([own, passed(own, row_even)], axis=0)
    inner = passed(ab, row_odd)
    outer = passed(inner, [(d, d ^ GW) for d in range(count) if d // GW in (1, 2)])
    cd = jnp.where(edge_row, outer, inner)
    pieces = {"ab": ab, "cd": cd}
    masks = {"ab": 0, "cd": 3 * GW}
    for bit, mark in ((2, "x"), (4, "y"), (1, "c")):
        for name in list(pieces):
            pieces[mark + name] = swap(pieces[name], bit)
            masks[mark + name] = masks[name] ^ bit
    return list(pieces.values()), tuple(masks.values())


def use_pieces(count, shard):
    return count == 4 * GW and shard % 16 == 0 and count % (128 // math.gcd(128, shard)) == 0


def local(queries, keys_values, tile_visible, out_weight):
    count = lax.axis_size("wa")
    grid_rows = count // GW
    me = lax.axis_index("wa")
    row, col = me // GW, me % GW
    time_tiles, _, width = queries.shape[1:]
    shard = out_weight.shape[1]

    row_even, row_odd = (pair_swaps(count, GW, parity, grid_rows) for parity in (0, 1))
    col_even, col_odd = (pair_swaps(count, 1, parity, GW) for parity in (0, 1))

    def partner(position, parity, limit):
        near = jnp.where(position % 2 == parity, position + 1, position - 1)
        return jnp.clip(near, 0, limit - 1), (near >= 0) & (near < limit)

    near_even, inside_even = partner(row, 0, grid_rows)
    near_odd, inside_odd = partner(row, 1, grid_rows)

    spread = use_pieces(count, shard)
    if spread:
        pieces, masks = gather_weight(out_weight.T, count, row_even, row_odd, (row == 0) | (row == 3))
    else:
        whole = lax.all_gather(out_weight, "wa", axis=1, tiled=True)

    head_count = width // HEAD_DIM
    chunks = [head_count // CHUNKS + (j < head_count % CHUNKS) for j in range(CHUNKS)]
    outputs = []
    for t in range(time_tiles):
        marked = tile_visible[:, t]
        flags = jnp.stack(
            [
                jnp.int32(1),
                (marked[me] == 1).astype(jnp.int32),
                (inside_even & (marked[near_even * GW + col] == 1)).astype(jnp.int32),
                (inside_odd & (marked[near_odd * GW + col] == 1)).astype(jnp.int32),
            ]
        )
        query = queries[0, t]
        kv_own = keys_values[:, 0, t]
        near_queries = [passed(query, col_even), passed(query, col_odd)]
        first = 0
        partial = []
        for heads in chunks:
            cut = kv_own[:, :, first * HEAD_DIM : (first + heads) * HEAD_DIM]
            kv_near = [passed(cut, row_even), passed(cut, row_odd)]
            partial.append((first, heads, kv_near))
            first += heads
        attended = []
        edge = (col == 0) | (col == GW - 1)
        for first, heads, kv_near in partial:
            own, even, odd = attend(flags, [query] + near_queries, kv_own, kv_near, first, heads)
            even = passed(even, col_even)
            odd = passed(odd, col_odd)
            attended.append(merge(edge.astype(jnp.int32).reshape(1), own, even, odd))
        if spread:
            outputs.append(project(attended, pieces, masks, shard, count))
        else:
            outputs.append(
                jnp.dot(
                    jnp.concatenate(attended, axis=1), whole, preferred_element_type=jnp.float32
                ).astype(jnp.bfloat16)
            )
    return jnp.stack(outputs)[None]


def solution(mesh):
    in_specs = (
        P(("groups", "wa"), None, None, None),
        P(None, ("groups", "wa"), None, None, None),
        P("groups", None),
        P(None, "wa"),
    )
    out_specs = P(("groups", "wa"), None, None, None)

    return jax.shard_map(local, mesh=mesh, in_specs=in_specs, out_specs=out_specs, check_vma=False)
```

```python
import functools
import math

import jax
import jax.numpy as jnp
from jax import lax
from jax.experimental import pallas as pl
from jax.experimental.pallas import tpu as pltpu
from jax.sharding import PartitionSpec as P


HEAD_DIM = 128
GW = 8
SHARES = (4, 4, 4)
STAT_ROWS = 16
VMEM_LIMIT = 67043328
STEP_HEADS = 2
BIG = 1e30


def pair_swaps(count, stride, parity, block):
    pairs = []
    for device in range(count):
        position = (device // stride) % block
        if position % 2 == parity % 2 and position + 1 < block:
            pairs.append((device, device + stride))
            pairs.append((device + stride, device))
    return pairs


def split_three(value):
    high = value.astype(jnp.bfloat16).astype(jnp.float32)
    rest = value - high
    middle = rest.astype(jnp.bfloat16).astype(jnp.float32)
    return [high, middle, rest - middle]


def attend_kernel(time_tile, grid_rows, own_row, visible, *refs):
    queries, outs = refs[:3], refs[-3:]
    windows, before = (refs[3:4], None) if own_row else (refs[3:5], refs[5:8])
    tile = queries[0].shape[0]
    me = lax.axis_index("wa")
    row, col = me // GW, lax.rem(me, GW)

    def marked(parity):
        near = jnp.where(lax.rem(row, 2) == parity, row + 1, row - 1)
        inside = (near >= 0) & (near < grid_rows)
        return inside & (visible[jnp.clip(near, 0, grid_rows - 1) * GW + col, time_tile] == 1)

    near_seen = None if own_row else (marked(0), marked(1))
    own_seen = visible[me, time_tile] == 1
    factor = HEAD_DIM ** (-0.5) * math.log2(math.e)
    unit = HEAD_DIM + STAT_ROWS

    @functools.cache
    def window(h):
        cols = slice(h * HEAD_DIM, (h + 1) * HEAD_DIM)
        keys = jnp.concatenate([kv[0, :, cols] for kv in windows], axis=0)
        values = jnp.concatenate([kv[1, :, cols].T for kv in windows], axis=1)
        return keys, jnp.concatenate([values, jnp.ones((STAT_ROWS, values.shape[1]), values.dtype)], axis=0)

    def score(h, place):
        query = queries[place][:, h * HEAD_DIM : (h + 1) * HEAD_DIM]
        return lax.dot_general(window(h)[0], query, (((1,), (1,)), ((), ())), preferred_element_type=jnp.float32)

    def finish(h, place, scores):
        body, tail = slice(h * unit, h * unit + HEAD_DIM), slice(h * unit + HEAD_DIM, (h + 1) * unit)
        seen = near_seen if near_seen is not None else (place == 0 or own_seen,)
        parts = [scores[t * tile : (t + 1) * tile] for t in range(len(windows))]
        peaks = [
            jnp.where(seen[t], jnp.max(part, axis=0, keepdims=True) * factor, -BIG) for t, part in enumerate(parts)
        ]
        if before is not None:
            stat = before[place][tail, :].astype(jnp.float32)
            peaks.append(stat[0:1] + stat[1:2] + stat[2:3])
        peak = functools.reduce(jnp.maximum, peaks)
        weights = [jnp.exp2(part * factor - jnp.where(seen[t], peak, BIG)) for t, part in enumerate(parts)]
        low = jnp.concatenate([w.astype(jnp.bfloat16) for w in weights], axis=0)
        summed = jnp.dot(window(h)[1], low, preferred_element_type=jnp.float32)
        total = summed[HEAD_DIM : HEAD_DIM + 1]
        summed = summed[:HEAD_DIM]
        if before is not None:
            share = jnp.exp2(peaks[-1] - peak)
            total = total + share
            summed = summed + before[place][body, :].astype(jnp.float32) * share
        some = total > 0.0
        safe = jnp.where(some, total, 1.0)
        level = jnp.where(some, peak + jnp.log2(safe), -BIG)
        outs[place][body, :] = (summed * (1.0 / safe)).astype(jnp.bfloat16)
        stats = split_three(level) + [jnp.zeros((STAT_ROWS - 3, tile), jnp.float32)]
        outs[place][tail, :] = jnp.concatenate(stats, axis=0).astype(jnp.bfloat16)

    order = [(h, place) for h in range(queries[0].shape[1] // HEAD_DIM) for place in range(3)]
    ahead = score(*order[0])
    for n, item in enumerate(order):
        scores = ahead
        if n + 1 < len(order):
            ahead = score(*order[n + 1])
        finish(*item, scores)


def attend(visible, time_tile, grid_rows, queries, windows, before, first_head, heads):
    tile = queries[0].shape[0]
    unit = HEAD_DIM + STAT_ROWS
    pair_count = 3 * tile * tile * heads * len(windows)
    few = math.gcd(math.gcd(heads, first_head), STEP_HEADS)
    first = first_head // few
    width = few * HEAD_DIM
    return pl.pallas_call(
        functools.partial(attend_kernel, time_tile, grid_rows, len(windows) == 1),
        grid_spec=pltpu.PrefetchScalarGridSpec(
            num_scalar_prefetch=1,
            grid=(heads // few,),
            in_specs=[pl.BlockSpec((tile, width), lambda h, f: (0, first + h))] * 3
            + [pl.BlockSpec((2, tile, width), lambda h, f: (0, 0, h))] * len(windows)
            + [pl.BlockSpec((few * unit, tile), lambda h, f: (first + h, 0))] * len(before),
            out_specs=[pl.BlockSpec((few * unit, tile), lambda h, f: (h, 0))] * 3,
        ),
        out_shape=[jax.ShapeDtypeStruct((heads * unit, tile), jnp.bfloat16)] * 3,
        cost_estimate=pl.CostEstimate(
            flops=pair_count * HEAD_DIM * 4,
            transcendentals=pair_count,
            bytes_accessed=heads * HEAD_DIM * tile * 2 * (6 + 2 * len(windows) + len(before)),
        ),
        compiler_params=pltpu.CompilerParams(vmem_limit_bytes=VMEM_LIMIT),
        name="attend",
    )(visible, *queries, *windows, *before)


def merge_head(parts, base, alone):
    levels = []
    for part in parts:
        stat = part[base + HEAD_DIM : base + HEAD_DIM + STAT_ROWS, :].astype(jnp.float32)
        levels.append(stat[0:1] + stat[1:2] + stat[2:3])
    levels[2] = jnp.where(alone, -BIG, levels[2])
    top = jnp.maximum(jnp.maximum(levels[0], levels[1]), levels[2])
    shares = [jnp.exp2(level - top) for level in levels]
    scale = 1.0 / (shares[0] + shares[1] + shares[2])
    mixed = None
    for part, share in zip(parts, shares):
        term = part[base : base + HEAD_DIM, :].astype(jnp.float32) * (share * scale)
        mixed = term if mixed is None else mixed + term
    return mixed


def alone_in_pairs():
    col = lax.rem(lax.axis_index("wa"), GW)
    return (col == 0) | (col == GW - 1)


def merge_kernel(*refs):
    attended = refs[-1]
    alone = alone_in_pairs()
    unit = HEAD_DIM + STAT_ROWS
    first = 0
    for j in range(0, len(refs) - 1, 3):
        for h in range(refs[j].shape[0] // unit):
            mixed = merge_head(refs[j : j + 3], h * unit, alone)
            attended[:, (first + h) * HEAD_DIM : (first + h + 1) * HEAD_DIM] = mixed.T.astype(jnp.bfloat16)
        first += refs[j].shape[0] // unit


def merge(partial):
    heads = sum(p.shape[0] for p in partial[::3]) // (HEAD_DIM + STAT_ROWS)
    return pl.pallas_call(
        merge_kernel,
        out_shape=jax.ShapeDtypeStruct((partial[0].shape[1], heads * HEAD_DIM), jnp.bfloat16),
        compiler_params=pltpu.CompilerParams(vmem_limit_bytes=VMEM_LIMIT),
        cost_estimate=pl.CostEstimate(
            flops=heads * partial[0].size, transcendentals=0, bytes_accessed=8 * heads * HEAD_DIM * partial[0].shape[1]
        ),
        name="merge",
    )(*partial)


def project_kernel(masks, shard, group, *refs):
    count = len(masks)
    pieces = refs[:count]
    early, partial = refs[count], refs[count + 1 : count + 4]
    out_ref, held, parts, attended, weight_sem, part_sem = refs[-6:]
    step = pl.program_id(0)
    me = lax.axis_index("wa")
    row = me // GW
    flip = jnp.where((row == 0) | (row == 3), GW, 0)
    unit = HEAD_DIM + STAT_ROWS
    ready = early.shape[1]

    def move(ref, place, owner):
        target = pl.ds(pl.multiple_of(owner * shard, shard), shard)
        return pltpu.make_async_copy(ref.at[pl.ds(place * shard, shard)], held.at[target], weight_sem.at[owner])

    @pl.when(step == 0)
    def _():
        copies = [pltpu.make_async_copy(ref, parts.at[i], part_sem.at[i]) for i, ref in enumerate(partial)]
        copies.append(pltpu.make_async_copy(early, attended.at[:, pl.ds(0, ready)], part_sem.at[3]))
        for one in copies:
            one.start()
        for ref, mask in zip(pieces, masks):
            first = jnp.bitwise_xor(me, mask)
            if mask & (2 * GW):
                first = jnp.bitwise_xor(first, flip)
            for place in range(2):
                move(ref, place, jnp.bitwise_xor(first, place * GW)).start()
        for one in copies:
            one.wait()
        alone = alone_in_pairs()
        for h in range(parts.shape[1] // unit):
            mixed = merge_head([parts.at[i] for i in range(3)], h * unit, alone)
            start = ready + h * HEAD_DIM
            attended[:, start : start + HEAD_DIM] = mixed.T.astype(jnp.bfloat16)

    for i in range(group):
        move(pieces[0], 0, step * group + i).wait()
    columns = pl.ds(pl.multiple_of(step * (group * shard), 128), group * shard)
    out_ref[...] = lax.dot_general(
        attended[...], held[columns, :], (((1,), (1,)), ((), ())), preferred_element_type=jnp.float32
    ).astype(jnp.bfloat16)


def weight_group(shard):
    return 256 // math.gcd(256, shard)


def project(early, partial, pieces, masks, shard, count):
    tile = partial[0].shape[1]
    depth = pieces[0].shape[1]
    group = weight_group(shard)
    return pl.pallas_call(
        functools.partial(project_kernel, masks, shard, group),
        grid=(count // group,),
        in_specs=[pl.BlockSpec(memory_space=pl.ANY)] * (len(pieces) + 4),
        out_specs=pl.BlockSpec((tile, group * shard), lambda g: (0, g)),
        out_shape=jax.ShapeDtypeStruct((tile, count * shard), jnp.bfloat16),
        scratch_shapes=[
            pltpu.VMEM((count * shard, depth), jnp.bfloat16),
            pltpu.VMEM((3, *partial[0].shape), jnp.bfloat16),
            pltpu.VMEM((tile, depth), jnp.bfloat16),
            pltpu.SemaphoreType.DMA((count,)),
            pltpu.SemaphoreType.DMA((4,)),
        ],
        cost_estimate=pl.CostEstimate(
            flops=2 * tile * depth * count * shard, transcendentals=0, bytes_accessed=2 * depth * count * shard
        ),
        compiler_params=pltpu.CompilerParams(vmem_limit_bytes=VMEM_LIMIT),
        name="project",
    )(*pieces, early, *partial)


def passed(value, pairs):
    return lax.ppermute(value, "wa", pairs)


def gather_weight(own, count, row_even, row_odd, edge_row):
    def swap(value, bit):
        return passed(value, [(device, device ^ bit) for device in range(count)])

    ab = jnp.concatenate([own, passed(own, row_even)], axis=0)
    inner = passed(ab, row_odd)
    outer = passed(inner, [(d, d ^ GW) for d in range(count) if d // GW in (1, 2)])
    cd = jnp.where(edge_row, outer, inner)
    pieces = {"ab": ab, "cd": cd}
    masks = {"ab": 0, "cd": 3 * GW}
    for bit, mark in ((2, "x"), (4, "y"), (1, "c")):
        for name in list(pieces):
            pieces[mark + name] = swap(pieces[name], bit)
            masks[mark + name] = masks[name] ^ bit
    return list(pieces.values()), tuple(masks.values())


def use_pieces(count, shard):
    return count == 4 * GW and shard % 16 == 0 and count % weight_group(shard) == 0


def local(queries, keys_values, tile_visible, out_weight):
    count = lax.axis_size("wa")
    grid_rows = count // GW
    row = lax.axis_index("wa") // GW
    time_tiles, _, width = queries.shape[1:]
    shard = out_weight.shape[1]

    row_even, row_odd = (pair_swaps(count, GW, parity, grid_rows) for parity in (0, 1))
    col_even, col_odd = (pair_swaps(count, 1, parity, GW) for parity in (0, 1))

    spread = use_pieces(count, shard)
    if spread:
        pieces, masks = gather_weight(out_weight.T, count, row_even, row_odd, (row == 0) | (row == 3))
    else:
        whole = lax.all_gather(out_weight, "wa", axis=1, tiled=True)

    head_count = width // HEAD_DIM
    chunks = [round(head_count * share / sum(SHARES)) for share in SHARES[:-1]]
    chunks.append(head_count - sum(chunks))
    outputs = []
    for t in range(time_tiles):
        query = queries[0, t]
        kv_own = keys_values[:, 0, t]
        near_queries = [passed(query, col_even), passed(query, col_odd)]
        first = 0
        partial = []
        for heads in chunks:
            cut = kv_own[:, :, first * HEAD_DIM : (first + heads) * HEAD_DIM]
            kv_near = [passed(cut, row_even), passed(cut, row_odd)]
            partial.append((first, heads, kv_near))
            first += heads
        results = []
        near_queries = [query] + near_queries
        before = attend(tile_visible, t, grid_rows, near_queries, [kv_own], [], 0, head_count)
        for first, heads, kv_near in partial:
            own, even, odd = attend(
                tile_visible, t, grid_rows, near_queries, kv_near, before, first, heads
            )
            results += [own, passed(even, col_even), passed(odd, col_odd)]
        if spread:
            early = merge(results[:-3])
            outputs.append(project(early, results[-3:], pieces, masks, shard, count))
        else:
            outputs.append(jnp.dot(merge(results), whole, preferred_element_type=jnp.float32).astype(jnp.bfloat16))
    return jnp.stack(outputs)[None]


def solution(mesh):
    in_specs = (
        P(("groups", "wa"), None, None, None),
        P(None, ("groups", "wa"), None, None, None),
        P("groups", None),
        P(None, "wa"),
    )
    out_specs = P(("groups", "wa"), None, None, None)

    return jax.shard_map(local, mesh=mesh, in_specs=in_specs, out_specs=out_specs, check_vma=False)
```

```python
import functools
import math

import jax
import jax.numpy as jnp
from jax import lax
from jax.experimental import pallas as pl
from jax.experimental.pallas import tpu as pltpu
from jax.sharding import PartitionSpec as P


HEAD_DIM = 128
GW = 8
SHARES = (6, 4, 2)
STAT_ROWS = 8
VMEM_LIMIT = 23068672
STEP_HEADS = 2
BIG = 1e30


def pair_swaps(count, stride, parity, block):
    pairs = []
    for device in range(count):
        position = (device // stride) % block
        if position % 2 == parity % 2 and position + 1 < block:
            pairs.append((device, device + stride))
            pairs.append((device + stride, device))
    return pairs


def split_three(value):
    high = value.astype(jnp.bfloat16).astype(jnp.float32)
    rest = value - high
    middle = rest.astype(jnp.bfloat16).astype(jnp.float32)
    return [high, middle, rest - middle]


def attend_kernel(time_tile, grid_rows, own_row, visible, *refs):
    queries, outs = refs[:3], refs[-3:]
    windows, before = (refs[3:4], None) if own_row else (refs[3:5], refs[5:8])
    tile = queries[0].shape[0]
    me = lax.axis_index("wa")
    row, col = me // GW, lax.rem(me, GW)

    def marked(parity):
        near = jnp.where(lax.rem(row, 2) == parity, row + 1, row - 1)
        inside = (near >= 0) & (near < grid_rows)
        return inside & (visible[jnp.clip(near, 0, grid_rows - 1) * GW + col, time_tile] == 1)

    near_seen = None if own_row else (marked(0), marked(1))
    own_seen = visible[me, time_tile] == 1
    factor = HEAD_DIM ** (-0.5) * math.log2(math.e)
    unit = HEAD_DIM + STAT_ROWS

    @functools.cache
    def window(h):
        cols = slice(h * HEAD_DIM, (h + 1) * HEAD_DIM)
        keys = jnp.concatenate([kv[0, :, cols] for kv in windows], axis=0)
        values = jnp.concatenate([kv[1, :, cols].T for kv in windows], axis=1)
        return keys, jnp.concatenate([values, jnp.ones((STAT_ROWS, values.shape[1]), values.dtype)], axis=0)

    def score(h, place):
        query = queries[place][:, h * HEAD_DIM : (h + 1) * HEAD_DIM]
        return lax.dot_general(window(h)[0], query, (((1,), (1,)), ((), ())), preferred_element_type=jnp.float32)

    def finish(h, place, scores):
        body, tail = slice(h * unit, h * unit + HEAD_DIM), slice(h * unit + HEAD_DIM, (h + 1) * unit)
        seen = near_seen if near_seen is not None else (place == 0 or own_seen,)
        parts = [scores[t * tile : (t + 1) * tile] for t in range(len(windows))]
        peaks = [
            jnp.where(seen[t], jnp.max(part, axis=0, keepdims=True) * factor, -BIG) for t, part in enumerate(parts)
        ]
        if before is not None:
            stat = before[place][tail, :].astype(jnp.float32)
            peaks.append(stat[0:1] + stat[1:2] + stat[2:3])
        peak = functools.reduce(jnp.maximum, peaks)
        weights = [jnp.exp2(part * factor - jnp.where(seen[t], peak, BIG)) for t, part in enumerate(parts)]
        low = jnp.concatenate([w.astype(jnp.bfloat16) for w in weights], axis=0)
        summed = jnp.dot(window(h)[1], low, preferred_element_type=jnp.float32)
        total = summed[HEAD_DIM : HEAD_DIM + 1]
        summed = summed[:HEAD_DIM]
        if before is not None:
            share = jnp.exp2(peaks[-1] - peak)
            total = total + share
            summed = summed + before[place][body, :].astype(jnp.float32) * share
        some = total > 0.0
        safe = jnp.where(some, total, 1.0)
        level = jnp.where(some, peak + jnp.log2(safe), -BIG)
        outs[place][body, :] = (summed * (1.0 / safe)).astype(jnp.bfloat16)
        stats = split_three(level) + [jnp.zeros((STAT_ROWS - 3, tile), jnp.float32)]
        outs[place][tail, :] = jnp.concatenate(stats, axis=0).astype(jnp.bfloat16)

    order = [(h, place) for h in range(queries[0].shape[1] // HEAD_DIM) for place in range(3)]
    ahead = score(*order[0])
    for n, item in enumerate(order):
        scores = ahead
        if n + 1 < len(order):
            ahead = score(*order[n + 1])
        finish(*item, scores)


def attend(visible, time_tile, grid_rows, queries, windows, before, first_head, heads):
    tile = queries[0].shape[0]
    unit = HEAD_DIM + STAT_ROWS
    pair_count = 3 * tile * tile * heads * len(windows)
    few = math.gcd(math.gcd(heads, first_head), STEP_HEADS)
    first = first_head // few
    width = few * HEAD_DIM
    return pl.pallas_call(
        functools.partial(attend_kernel, time_tile, grid_rows, len(windows) == 1),
        grid_spec=pltpu.PrefetchScalarGridSpec(
            num_scalar_prefetch=1,
            grid=(heads // few,),
            in_specs=[pl.BlockSpec((tile, width), lambda h, f: (0, first + h))] * 3
            + [pl.BlockSpec((2, tile, width), lambda h, f: (0, 0, h))] * len(windows)
            + [pl.BlockSpec((few * unit, tile), lambda h, f: (first + h, 0))] * len(before),
            out_specs=[pl.BlockSpec((few * unit, tile), lambda h, f: (h, 0))] * 3,
        ),
        out_shape=[jax.ShapeDtypeStruct((heads * unit, tile), jnp.bfloat16)] * 3,
        cost_estimate=pl.CostEstimate(
            flops=pair_count * HEAD_DIM * 4,
            transcendentals=pair_count,
            bytes_accessed=heads * HEAD_DIM * tile * 2 * (6 + 2 * len(windows) + len(before)),
        ),
        compiler_params=pltpu.CompilerParams(vmem_limit_bytes=VMEM_LIMIT),
        name="attend",
    )(visible, *queries, *windows, *before)


def merge_head(parts, base, alone):
    levels = []
    for part in parts:
        stat = part[base + HEAD_DIM : base + HEAD_DIM + STAT_ROWS, :].astype(jnp.float32)
        levels.append(stat[0:1] + stat[1:2] + stat[2:3])
    levels[2] = jnp.where(alone, -BIG, levels[2])
    top = jnp.maximum(jnp.maximum(levels[0], levels[1]), levels[2])
    shares = [jnp.exp2(level - top) for level in levels]
    scale = 1.0 / (shares[0] + shares[1] + shares[2])
    mixed = None
    for part, share in zip(parts, shares):
        term = part[base : base + HEAD_DIM, :].astype(jnp.float32) * (share * scale)
        mixed = term if mixed is None else mixed + term
    return mixed


def alone_in_pairs():
    col = lax.rem(lax.axis_index("wa"), GW)
    return (col == 0) | (col == GW - 1)


def merge_kernel(*refs):
    attended = refs[-1]
    alone = alone_in_pairs()
    unit = HEAD_DIM + STAT_ROWS
    first = 0
    for j in range(0, len(refs) - 1, 3):
        for h in range(refs[j].shape[0] // unit):
            mixed = merge_head(refs[j : j + 3], h * unit, alone)
            attended[:, (first + h) * HEAD_DIM : (first + h + 1) * HEAD_DIM] = mixed.T.astype(jnp.bfloat16)
        first += refs[j].shape[0] // unit


def merge(partial):
    heads = sum(p.shape[0] for p in partial[::3]) // (HEAD_DIM + STAT_ROWS)
    return pl.pallas_call(
        merge_kernel,
        out_shape=jax.ShapeDtypeStruct((partial[0].shape[1], heads * HEAD_DIM), jnp.bfloat16),
        compiler_params=pltpu.CompilerParams(vmem_limit_bytes=VMEM_LIMIT),
        cost_estimate=pl.CostEstimate(
            flops=heads * partial[0].size, transcendentals=0, bytes_accessed=8 * heads * HEAD_DIM * partial[0].shape[1]
        ),
        name="merge",
    )(*partial)


def project_kernel(masks, shard, group, *refs):
    count = len(masks)
    pieces = refs[:count]
    early, partial = refs[count], refs[count + 1 : count + 4]
    out_ref, held, parts, attended, weight_sem, part_sem = refs[-6:]
    step = pl.program_id(0)
    me = lax.axis_index("wa")
    row = me // GW
    flip = jnp.where((row == 0) | (row == 3), GW, 0)
    unit = HEAD_DIM + STAT_ROWS
    ready = early.shape[1]

    def move(ref, place, owner):
        target = pl.ds(pl.multiple_of(owner * shard, shard), shard)
        return pltpu.make_async_copy(ref.at[pl.ds(place * shard, shard)], held.at[target], weight_sem.at[owner])

    @pl.when(step == 0)
    def _():
        copies = [pltpu.make_async_copy(ref, parts.at[i], part_sem.at[i]) for i, ref in enumerate(partial)]
        copies.append(pltpu.make_async_copy(early, attended.at[:, pl.ds(0, ready)], part_sem.at[3]))
        for one in copies:
            one.start()
        for ref, mask in zip(pieces, masks):
            first = jnp.bitwise_xor(me, mask)
            if mask & (2 * GW):
                first = jnp.bitwise_xor(first, flip)
            for place in range(2):
                move(ref, place, jnp.bitwise_xor(first, place * GW)).start()
        for one in copies:
            one.wait()
        alone = alone_in_pairs()
        for h in range(parts.shape[1] // unit):
            mixed = merge_head([parts.at[i] for i in range(3)], h * unit, alone)
            start = ready + h * HEAD_DIM
            attended[:, start : start + HEAD_DIM] = mixed.T.astype(jnp.bfloat16)

    for i in range(group):
        move(pieces[0], 0, step * group + i).wait()
    columns = pl.ds(pl.multiple_of(step * (group * shard), 128), group * shard)
    out_ref[...] = lax.dot_general(
        attended[...], held[columns, :], (((1,), (1,)), ((), ())), preferred_element_type=jnp.float32
    ).astype(jnp.bfloat16)


def weight_group(shard):
    return 256 // math.gcd(256, shard)


def project(early, partial, pieces, masks, shard, count):
    tile = partial[0].shape[1]
    depth = pieces[0].shape[1]
    group = weight_group(shard)
    return pl.pallas_call(
        functools.partial(project_kernel, masks, shard, group),
        grid=(count // group,),
        in_specs=[pl.BlockSpec(memory_space=pl.ANY)] * (len(pieces) + 4),
        out_specs=pl.BlockSpec((tile, group * shard), lambda g: (0, g)),
        out_shape=jax.ShapeDtypeStruct((tile, count * shard), jnp.bfloat16),
        scratch_shapes=[
            pltpu.VMEM((count * shard, depth), jnp.bfloat16),
            pltpu.VMEM((3, *partial[0].shape), jnp.bfloat16),
            pltpu.VMEM((tile, depth), jnp.bfloat16),
            pltpu.SemaphoreType.DMA((count,)),
            pltpu.SemaphoreType.DMA((4,)),
        ],
        cost_estimate=pl.CostEstimate(
            flops=2 * tile * depth * count * shard, transcendentals=0, bytes_accessed=2 * depth * count * shard
        ),
        compiler_params=pltpu.CompilerParams(vmem_limit_bytes=VMEM_LIMIT),
        name="project",
    )(*pieces, early, *partial)


def passed(value, pairs):
    return lax.ppermute(value, "wa", pairs)


def gather_weight(own, count, row_even, row_odd, edge_row):
    def swap(value, bit):
        return passed(value, [(device, device ^ bit) for device in range(count)])

    ab = jnp.concatenate([own, passed(own, row_even)], axis=0)
    inner = passed(ab, row_odd)
    outer = passed(inner, [(d, d ^ GW) for d in range(count) if d // GW in (1, 2)])
    cd = jnp.where(edge_row, outer, inner)
    pieces = {"ab": ab, "cd": cd}
    masks = {"ab": 0, "cd": 3 * GW}
    for bit, mark in ((2, "x"), (4, "y"), (1, "c")):
        for name in list(pieces):
            pieces[mark + name] = swap(pieces[name], bit)
            masks[mark + name] = masks[name] ^ bit
    return list(pieces.values()), tuple(masks.values())


def use_pieces(count, shard):
    return count == 4 * GW and shard % 16 == 0 and count % weight_group(shard) == 0


def local(queries, keys_values, tile_visible, out_weight):
    count = lax.axis_size("wa")
    grid_rows = count // GW
    row = lax.axis_index("wa") // GW
    time_tiles, _, width = queries.shape[1:]
    shard = out_weight.shape[1]

    row_even, row_odd = (pair_swaps(count, GW, parity, grid_rows) for parity in (0, 1))
    col_even, col_odd = (pair_swaps(count, 1, parity, GW) for parity in (0, 1))

    spread = use_pieces(count, shard)
    if spread:
        pieces, masks = gather_weight(out_weight.T, count, row_even, row_odd, (row == 0) | (row == 3))
    else:
        whole = lax.all_gather(out_weight, "wa", axis=1, tiled=True)

    head_count = width // HEAD_DIM
    chunks = [round(head_count * share / sum(SHARES)) for share in SHARES[:-1]]
    chunks.append(head_count - sum(chunks))
    outputs = []
    for t in range(time_tiles):
        query = queries[0, t]
        kv_own = keys_values[:, 0, t]
        near_queries = [passed(query, col_even), passed(query, col_odd)]
        first = 0
        partial = []
        for heads in chunks:
            cut = kv_own[:, :, first * HEAD_DIM : (first + heads) * HEAD_DIM]
            kv_near = [passed(cut, row_even), passed(cut, row_odd)]
            partial.append((first, heads, kv_near))
            first += heads
        results = []
        near_queries = [query] + near_queries
        before = attend(tile_visible, t, grid_rows, near_queries, [kv_own], [], 0, head_count)
        for first, heads, kv_near in partial:
            own, even, odd = attend(
                tile_visible, t, grid_rows, near_queries, kv_near, before, first, heads
            )
            results += [own, passed(even, col_even), passed(odd, col_odd)]
        if spread:
            early = merge(results[:-3])
            outputs.append(project(early, results[-3:], pieces, masks, shard, count))
        else:
            outputs.append(jnp.dot(merge(results), whole, preferred_element_type=jnp.float32).astype(jnp.bfloat16))
    return jnp.stack(outputs)[None]


def solution(mesh):
    in_specs = (
        P(("groups", "wa"), None, None, None),
        P(None, ("groups", "wa"), None, None, None),
        P("groups", None),
        P(None, "wa"),
    )
    out_specs = P(("groups", "wa"), None, None, None)

    return jax.shard_map(local, mesh=mesh, in_specs=in_specs, out_specs=out_specs, check_vma=False)
```
